32 devices in a mesh: ctx: 8 (over y, x, core), head: 4 (over z).
Axes of the slice: x: 2, y: 2, z: 4, core: 2. Of those that a mesh axis runs over, the one named last changes fastest.
Arguments:
- queries: bfloat16 [1024, 32, 576], P('ctx', 'head'), may hold values from -512 to 512
- latent: bfloat16 [1024, 576], P(('ctx', 'head')), may hold values from -6 to 6
- out_grad: bfloat16 [1024, 32, 512], P('ctx', 'head'), may hold values from -6 to 6
- segments: int32 [1024], replicated, may hold values from 0 to 3, never falling along the last dimension, each value on 1 to 512 neighbouring positions
Outputs:
- query_grad: bfloat16 [1024, 32, 576], P('ctx', 'head')
- latent_grad: float32 [1024, 576], P(('ctx', 'head'))
The draws below stay inside these ranges and needn't reach their ends.
All inputs are finite; a program needn't handle non-finite values.
Results may differ from the reference program's by a relative error of at most 0.018.
Values may be sent and summed in bfloat16 or wider, within the bound.
A program may use at most 64 MiB of HBM per device.

```python
import math
import jax
import jax.numpy as jnp
import numpy as np
from jax import lax

KV_RANK = 512
LAT = 576
HEADS = 32
Q_DEV = 128
WINDOW = 4
TOKENS = 1024
N_CTX = 8


def latent_field(key):
    inner = jax.random.fold_in(key, 7)
    values = jax.random.truncated_normal(inner, -6.0, 6.0, (TOKENS, LAT), jnp.float32)
    return values.astype(jnp.bfloat16).astype(jnp.float32)


def draw_latent(key, part):
    return latent_field(key).astype(jnp.bfloat16)


def draw_queries(key, part):
    inner = jax.random.fold_in(key, 11)
    values = jax.random.truncated_normal(inner, -6.0, 6.0, (TOKENS, HEADS, LAT), jnp.float32)
    return values.astype(jnp.bfloat16)


def steps_of(own_key, shape, pieces, low, top_value):
    def one(position, blocks):
        draws = jax.random.uniform(jax.random.fold_in(jax.random.fold_in(own_key, 6), position), (blocks,), jnp.float32, low / len(pieces), top_value / len(pieces))
        return jnp.repeat(jnp.exp(draws), shape[position] // blocks).reshape((-1,) + (1,) * (len(shape) - position - 1))

    gain = one(*pieces[0])
    for cut in pieces[1:]:
        gain = gain * one(*cut)
    return gain


def profile(count, total, reach, skew):
    loads = [(1 << 20) // math.isqrt(grade ** skew) + 1 for grade in range(2, count + 1)]
    spare, counts = total - reach - (count - 1), [1] * (count - 1)
    while spare > 0:
        candidates = [i for i in range(count - 1) if counts[i] < reach]
        pool, remaining = sum([loads[i] for i in candidates]), spare
        for i in candidates:
            addition = min(reach - counts[i], max(1, remaining * loads[i] // pool), spare)
            counts[i] = counts[i] + addition
            spare = spare - addition
    return np.array([reach] + counts)


def ragged_sizes(key, number_of, total, reach, slope):
    if number_of == 2:
        one = jax.random.randint(key, (), max(1, total - reach), min(reach, total - 1) + 1)
        return jnp.stack([one, total - one])
    lengths = jnp.asarray(profile(number_of, total, reach, slope), jnp.int32)
    pairs = (number_of - 1) // 2
    source_of, taker = lengths[1:1 + 2 * pairs:2], lengths[2:2 + 2 * pairs:2]
    slack = jnp.minimum(source_of - 1, reach - taker)
    passed = jax.random.randint(jax.random.fold_in(key, 1), (pairs,), 0, 1 << 20) % (slack + 1)
    lengths = lengths.at[1:1 + 2 * pairs:2].set(source_of - passed).at[2:2 + 2 * pairs:2].set(taker + passed)
    return lengths[jax.random.permutation(jax.random.fold_in(key, 2), number_of)]


def gaussian(rng, dims, width, most, pieces=(), held_as=jnp.bfloat16):
    loudness = steps_of(rng, dims, pieces, -0.22, 0.18) if pieces else 1.0
    result = jax.random.normal(rng, dims, jnp.float32) * width * loudness
    return jnp.minimum(jnp.maximum(result, -most), most).astype(held_as)


def setup_inputs(seed: int = 0) -> dict:
    splits = jax.random.split(jax.random.key(seed), 5)
    queries = draw_queries(jax.random.fold_in(splits[4], 71), 0)
    latent = draw_latent(jax.random.fold_in(splits[4], 71), 0)
    out_grad = gaussian(splits[2], (TOKENS, HEADS, KV_RANK), 1.0, 6.0, ((0, 8), (1, 4)))
    segments = jnp.searchsorted(jnp.cumsum(ragged_sizes(splits[3], TOKENS // (2 * Q_DEV), TOKENS, WINDOW * Q_DEV, 0)), jnp.arange(TOKENS), side="right").astype(jnp.int32)
    return {"queries": queries, "latent": latent, "out_grad": out_grad, "segments": segments}


score_scale = 192.0 ** -0.5


def window_mask(query_index, key_index, query_segments, key_segments):
    causal = (key_index[None, :] >= 0) & (key_index[None, :] <= query_index[:, None])
    return causal & (key_segments[None, :] == query_segments[:, None])


def block_grads(query_rows, key_rows, grad_rows, allowed_mask):
    head_count = query_rows.shape[1]
    value_rank = grad_rows.shape[2]
    query_flat = query_rows.reshape(-1, query_rows.shape[2])
    grad_flat = grad_rows.reshape(-1, value_rank)
    inner_dims = (((1,), (1,)), ((), ()))
    outer_dims = (((0,), (0,)), ((), ()))
    scores = score_scale * lax.dot_general(query_flat, key_rows, inner_dims, preferred_element_type=jnp.float32)
    expanded = jnp.repeat(allowed_mask, head_count, axis=0)
    scores = jnp.where(expanded, scores, -1e30)
    row_max = jnp.max(scores, axis=1, keepdims=True)
    weights = jnp.where(expanded, jnp.exp(scores - row_max), 0.0)
    soft_probs = weights / jnp.sum(weights, axis=1, keepdims=True)
    probs_half = soft_probs.astype(jnp.bfloat16)
    grad_probs = lax.dot_general(grad_flat, key_rows[:, :value_rank], inner_dims, preferred_element_type=jnp.float32)
    row_delta = jnp.sum(soft_probs * grad_probs, axis=1, keepdims=True)
    grad_scores = (soft_probs * (grad_probs - row_delta)).astype(jnp.bfloat16)
    grad_query = (score_scale * jnp.dot(grad_scores, key_rows, preferred_element_type=jnp.float32)).astype(jnp.bfloat16)
    from_scores = lax.dot_general(grad_scores, query_flat, outer_dims, preferred_element_type=jnp.float32)
    from_values = lax.dot_general(probs_half, grad_flat, outer_dims, preferred_element_type=jnp.float32)
    rope_zeros = jnp.zeros((from_values.shape[0], key_rows.shape[1] - value_rank), jnp.float32)
    grad_keys = score_scale * from_scores + jnp.concatenate([from_values, rope_zeros], axis=1)
    return grad_query.reshape(query_rows.shape), grad_keys


def reference(queries, latent, out_grad, segments):
    key_span = WINDOW * Q_DEV
    lead_rows = key_span - Q_DEV
    padded_latent = jnp.concatenate([jnp.zeros((lead_rows, LAT), latent.dtype), latent], axis=0)
    padded_segments = jnp.concatenate([jnp.full((lead_rows,), -1, jnp.int32), segments.astype(jnp.int32)])

    def visit(accum, block_idx):
        first_row = (block_idx * Q_DEV).astype(jnp.int32)
        query_rows = lax.dynamic_slice_in_dim(queries, first_row, Q_DEV, 0)
        grad_rows = lax.dynamic_slice_in_dim(out_grad, first_row, Q_DEV, 0)
        key_rows = lax.dynamic_slice_in_dim(padded_latent, first_row, key_span, 0)
        key_segments = lax.dynamic_slice_in_dim(padded_segments, first_row, key_span, 0)
        query_segments = lax.dynamic_slice_in_dim(segments.astype(jnp.int32), first_row, Q_DEV, 0)
        query_index = first_row + jnp.arange(Q_DEV, dtype=jnp.int32)
        key_index = first_row - lead_rows + jnp.arange(key_span, dtype=jnp.int32)
        allowed_mask = window_mask(query_index, key_index, query_segments, key_segments)
        grad_query, grad_keys = block_grads(query_rows, key_rows, grad_rows, allowed_mask)
        current = lax.dynamic_slice_in_dim(accum, first_row, key_span, 0)
        accum = lax.dynamic_update_slice_in_dim(accum, current + grad_keys, first_row, 0)
        return accum, grad_query

    start_accum = jnp.zeros((TOKENS + lead_rows, LAT), jnp.float32)
    key_total, query_grads = lax.scan(visit, start_accum, jnp.arange(N_CTX, dtype=jnp.int32))
    return query_grads.reshape(TOKENS, HEADS, LAT), key_total[lead_rows:]
```

```python
import functools

import jax
import jax.numpy as jnp
from jax import lax
from jax.experimental import pallas as pl
from jax.experimental.pallas import tpu as pltpu
from jax.sharding import PartitionSpec as P

WINDOW = 4
BACK3, BACK1, BACK2, OWN = 0, 1, 2, 3
DISTANCE = (3, 1, 2, 0)

score_scale = 192.0 ** (-0.5)


def when(cond):
    if cond is None:
        return lambda f: f()
    return pl.when(cond)


def flat(value, rows):
    if value.dtype == jnp.bfloat16 and value.shape[-2] % 16:
        return value.astype(jnp.float32).reshape(rows, value.shape[-1]).astype(jnp.bfloat16)
    return value.reshape(rows, value.shape[-1])


def kernel(
    n, heads, q_hbm, lat_ref, g_hbm, seg_ref, dq_hbm, dlat_ref,
    q3, g3, gw, qf, gf, kv, kf, kseg, allow, pt, dst, dk, sb, rp, r2, r3, zb, dq3,
    io_sem, g_send, g_recv, r_send, r_recv,
):
    c = lax.axis_index("ctx")
    h = lax.axis_index("head")
    odd = c % 2 == 1
    even = c % 2 == 0
    partner = (c + 1 - 2 * (c % 2), h)
    per, width, rows = q_hbm.shape
    rank = gf.shape[1]
    flat_rows = rows * per
    keys = WINDOW * rows
    f32, bf16 = jnp.float32, jnp.bfloat16

    def remote(src, dst_ref, ssem, rsem, peer):
        return pltpu.make_async_remote_copy(
            src_ref=src, dst_ref=dst_ref, send_sem=ssem, recv_sem=rsem,
            device_id=peer, device_id_type=pl.DeviceIdType.MESH,
        )

    def arrived(ref, sem):
        remote(ref, ref, sem, sem, partner).wait_recv()

    def sent(ref, sem):
        remote(ref, ref, sem, sem, partner).wait_send()

    load_q = pltpu.make_async_copy(q_hbm, q3, io_sem.at[0])
    load_g = pltpu.make_async_copy(g_hbm, g3, io_sem.at[1])
    load_g.start()
    load_q.start()

    up2, down2 = c + 2 < n, c >= 2
    up3, down3 = odd & (c + 3 < n), even & (c >= 3)
    peers = [(None, (c, (h + k) % heads)) for k in range(1, heads)]
    peers += [(None, partner), (up2, (c + 2, h)), (down2, (c - 2, h)),
              (up3, (c + 3, h)), (down3, (c - 3, h))]
    barrier = pltpu.get_barrier_semaphore()
    for cond, peer in peers:
        @when(cond)
        def _():
            pl.semaphore_signal(
                barrier, inc=1, device_id=peer, device_id_type=pl.DeviceIdType.MESH
            )
    flags = [cond for cond, _ in peers if cond is not None]
    pl.semaphore_wait(barrier, len(peers) - len(flags) + sum(f.astype(jnp.int32) for f in flags))

    def onward(src, s):
        @pl.when(up2)
        def _():
            remote(src, kv.at[BACK2, s], g_send.at[1, s], g_recv.at[BACK2, s], (c + 2, h)).start()

        @pl.when(up3)
        def _():
            remote(src, kv.at[BACK3, s], g_send.at[2, s], g_recv.at[BACK3, s], (c + 3, h)).start()

        @pl.when(even)
        def _():
            remote(src, kv.at[BACK1, s], g_send.at[2, s], g_recv.at[BACK1, s], partner).start()

    def relay(s):
        @pl.when(down2)
        def _():
            arrived(kv.at[BACK2, s], g_recv.at[BACK2, s])

            @pl.when(even)
            def _():
                remote(kv.at[BACK2, s], kv.at[BACK3, s], g_send.at[3, s], g_recv.at[BACK3, s], partner).start()

            @pl.when(odd)
            def _():
                remote(kv.at[BACK2, s], kv.at[BACK1, s], g_send.at[3, s], g_recv.at[BACK1, s], partner).start()

    for k in range(1, heads):
        remote(lat_ref, kv.at[OWN, h], g_send.at[0, k], g_recv.at[OWN, h], (c, (h + k) % heads)).start()
    onward(lat_ref, h)
    kv[OWN, h] = lat_ref[...]

    for place, cond in ((BACK1, c < 1), (BACK2, c < 2), (BACK3, c < 3)):
        @pl.when(cond)
        def _():
            kv[place] = jnp.zeros(kv.shape[1:], kv.dtype)

    load_g.wait()
    lanes = gw.shape[2]
    for i in range(rank // lanes):
        part = pl.ds(i * lanes, lanes)
        gw[i] = g3[:, :, part].astype(f32).reshape(flat_rows, lanes)
        for j in range(per):
            gf[pl.ds(j * rows, rows), part] = gw[i, pl.ds(j, rows, stride=per), :].astype(bf16)

    for k in range(1, heads):
        s = (h + heads - k) % heads
        arrived(kv.at[OWN, s], g_recv.at[OWN, s])
        onward(kv.at[OWN, s], s)
        relay((s + 1) % heads)
    relay((h + 1) % heads)

    load_q.wait()
    for j in range(per):
        qf[:, pl.ds(j * rows, rows)] = q3[j]

    for place, distance in enumerate(DISTANCE):
        row = seg_ref[pl.ds(jnp.maximum(c - distance, 0), 1), :].astype(f32)
        row = jnp.where(c >= distance, row, -1.0)
        kseg[pl.ds(place * rows, rows), :] = jnp.broadcast_to(row, (rows, rows)).T
    qseg = seg_ref[pl.ds(c, 1), :].astype(f32)
    key_at = lax.broadcasted_iota(jnp.int32, (keys, rows), 0) - OWN * rows
    token_at = lax.broadcasted_iota(jnp.int32, (keys, rows), 1)
    allow[...] = ((kseg[...] == qseg) & (key_at <= token_at)).astype(f32)

    for s in range(heads):
        @pl.when(c >= 1)
        def _():
            arrived(kv.at[BACK1, s], g_recv.at[BACK1, s])

        @pl.when(c >= 3)
        def _():
            arrived(kv.at[BACK3, s], g_recv.at[BACK3, s])
    kf[...] = flat(kv[...], keys)

    nt = (((1,), (1,)), ((), ()))
    tn = (((0,), (0,)), ((), ()))
    cols = rows * 2
    for start in range(0, flat_rows, cols):
        part = pl.ds(start, cols)
        st = score_scale * jnp.dot(kf[...], qf[:, part], preferred_element_type=f32)
        gt = lax.dot_general(kf[:, :rank], gf[part, :], nt, preferred_element_type=f32)
        allowed = jnp.concatenate([allow[...]] * (cols // rows), axis=1) > 0.0
        st = jnp.where(allowed, st, -1e30)
        top = jnp.max(st, axis=0, keepdims=True)
        w = jnp.where(allowed, jnp.exp(st - top), 0.0)
        probs = w * (1.0 / jnp.sum(w, axis=0, keepdims=True))
        pt[:, part] = probs.astype(bf16)
        delta = jnp.sum(probs * gt, axis=0, keepdims=True)
        dst[:, part] = (probs * (gt - delta)).astype(bf16)

    def key_grads(first):
        part = pl.ds(first * rows, 2 * rows)
        from_scores = lax.dot_general(dst[part, :], qf[...], nt, preferred_element_type=f32)
        from_values = jnp.dot(pt[part, :], gf[...], preferred_element_type=f32)
        total = jnp.concatenate(
            [score_scale * from_scores[:, :rank] + from_values, score_scale * from_scores[:, rank:]],
            axis=1,
        )
        dk[pl.ds(first, 2)] = total.reshape((2,) + dk.shape[1:])

    order = [(h + k) % heads for k in range(1, heads + 1)]
    key_grads(BACK3)
    sb[pl.ds(BACK3, 2)] = dk[pl.ds(BACK3, 2)].astype(bf16)
    for s in order:
        @pl.when(even & down2)
        def _():
            remote(sb.at[BACK1, s], rp.at[0, s], r_send.at[0, s], r_recv.at[0, s], partner).start()

        @pl.when(odd & (c >= 3))
        def _():
            remote(sb.at[BACK3, s], rp.at[0, s], r_send.at[0, s], r_recv.at[0, s], partner).start()

        @pl.when(odd)
        def _():
            remote(sb.at[BACK1, s], rp.at[1, s], r_send.at[1, s], r_recv.at[1, s], partner).start()

        @pl.when(down3)
        def _():
            remote(sb.at[BACK3, s], r3.at[s], r_send.at[1, s], r_recv.at[3, s], (c - 3, h)).start()
    key_grads(BACK2)
    for s in order:
        @pl.when(down2)
        def _():
            arrived(rp.at[0, s], r_recv.at[0, s])
            sb[BACK2, s] = (dk[BACK2, s] + rp[0, s].astype(f32)).astype(bf16)
            remote(sb.at[BACK2, s], r2.at[s], r_send.at[2, s], r_recv.at[2, s], (c - 2, h)).start()

    for start in range(0, flat_rows, cols):
        dq = score_scale * lax.dot_general(kf[...], dst[:, pl.ds(start, cols)], tn, preferred_element_type=f32)
        for j in range(cols // rows):
            dq3[start // rows + j] = dq[:, j * rows:(j + 1) * rows].astype(bf16)
    store_q = pltpu.make_async_copy(dq3, dq_hbm, io_sem.at[0])
    store_q.start()

    for k, s in enumerate(order):
        @pl.when(even)
        def _():
            arrived(rp.at[1, s], r_recv.at[1, s])
            dk[OWN, s] += rp[1, s].astype(f32)

        @pl.when(up2)
        def _():
            arrived(r2.at[s], r_recv.at[2, s])
            dk[OWN, s] += r2[s].astype(f32)

        @pl.when(up3)
        def _():
            arrived(r3.at[s], r_recv.at[3, s])
            dk[OWN, s] += r3[s].astype(f32)

        if k < heads - 1:
            sb[OWN, s] = dk[OWN, s].astype(bf16)
            remote(sb.at[OWN, s], zb.at[h], r_send.at[3, s], r_recv.at[4, h], (c, s)).start()
    total = dk[OWN, h]
    for s in order[-2::-1]:
        arrived(zb.at[s], r_recv.at[4, s])
        total = total + zb[s].astype(f32)
    dlat_ref[...] = total

    shard = zb.at[0]
    for k in range(1, heads):
        sent(lat_ref, g_send.at[0, k])
        sent(shard, r_send.at[3, order[k - 1]])
    for s in range(heads):
        for cond, sem in (
            (up2, g_send.at[1, s]), (up3, g_send.at[2, s]), (even, g_send.at[2, s]),
            (down2, g_send.at[3, s]), (even & down2, r_send.at[0, s]), (odd & (c >= 3), r_send.at[0, s]),
            (odd, r_send.at[1, s]), (down3, r_send.at[1, s]), (down2, r_send.at[2, s]),
        ):
            @pl.when(cond)
            def _():
                sent(shard, sem)
    store_q.wait()


def shards(n, heads, queries, latent, out_grad, segments):
    rows, per, width = queries.shape
    rank = out_grad.shape[2]
    height = latent.shape[0]
    f32, bf16 = jnp.float32, jnp.bfloat16
    flat_rows, keys = rows * per, WINDOW * rows
    vmem = pl.BlockSpec(memory_space=pltpu.VMEM)
    hbm = pl.BlockSpec(memory_space=pl.ANY)
    query_grad, latent_grad = pl.pallas_call(
        functools.partial(kernel, n, heads),
        out_shape=(
            jax.ShapeDtypeStruct((per, width, rows), bf16),
            jax.ShapeDtypeStruct(latent.shape, f32),
        ),
        in_specs=[hbm, vmem, hbm, vmem],
        out_specs=(hbm, vmem),
        scratch_shapes=[
            pltpu.VMEM((per, width, rows), bf16),
            pltpu.VMEM((rows, per, rank), bf16),
            pltpu.VMEM((rank // 128, flat_rows, 128), f32),
            pltpu.VMEM((width, flat_rows), bf16),
            pltpu.VMEM((flat_rows, rank), bf16),
            pltpu.VMEM((WINDOW, heads, height, width), bf16),
            pltpu.VMEM((keys, width), bf16),
            pltpu.VMEM((keys, rows), f32),
            pltpu.VMEM((keys, rows), f32),
            pltpu.VMEM((keys, flat_rows), bf16),
            pltpu.VMEM((keys, flat_rows), bf16),
            pltpu.VMEM((WINDOW, heads, height, width), f32),
            pltpu.VMEM((WINDOW, heads, height, width), bf16),
            pltpu.VMEM((2, heads, height, width), bf16),
            pltpu.VMEM((heads, height, width), bf16),
            pltpu.VMEM((heads, height, width), bf16),
            pltpu.VMEM((heads, height, width), bf16),
            pltpu.VMEM((per, width, rows), bf16),
            pltpu.SemaphoreType.DMA((2,)),
            pltpu.SemaphoreType.DMA((4, heads)),
            pltpu.SemaphoreType.DMA((4, heads)),
            pltpu.SemaphoreType.DMA((4, heads)),
            pltpu.SemaphoreType.DMA((5, heads)),
        ],
        compiler_params=pltpu.CompilerParams(
            collective_id=0, has_side_effects=True, vmem_limit_bytes=67043328
        ),
    )(queries.transpose(1, 2, 0), latent, out_grad, segments.reshape(-1, rows))
    return query_grad.transpose(2, 0, 1), latent_grad


def solution(mesh):
    n, heads = mesh.shape["ctx"], mesh.shape["head"]
    in_specs = (P("ctx", "head", None), P(("ctx", "head"), None), P("ctx", "head", None), P())
    out_specs = (P("ctx", "head", None), P(("ctx", "head"), None))
    return jax.shard_map(
        functools.partial(shards, n, heads),
        mesh=mesh, in_specs=in_specs, out_specs=out_specs, check_vma=False,
    )
```

```python
import functools

import jax
import jax.numpy as jnp
from jax import lax
from jax.experimental import pallas as pl
from jax.experimental.pallas import tpu as pltpu
from jax.sharding import PartitionSpec as P

WINDOW = 4
BACK3, BACK1, BACK2, OWN = 0, 1, 2, 3
DISTANCE = (3, 1, 2, 0)

score_scale = 192.0 ** (-0.5)


def when(cond):
    if cond is None:
        return lambda f: f()
    return pl.when(cond)


def flat(value, rows):
    if value.dtype == jnp.bfloat16 and value.shape[-2] % 16:
        return value.astype(jnp.float32).reshape(rows, value.shape[-1]).astype(jnp.bfloat16)
    return value.reshape(rows, value.shape[-1])


def kernel(
    n, heads, q_hbm, lat_ref, g_hbm, seg_ref, dq3, dlat_ref,
    q3, g3, gw, qf, gf, kv, kf, kseg, allow, pt, dst, dk, sb, rp, r2, r3, zb,
    io_sem, g_send, g_recv, r_send, r_recv,
):
    c = lax.axis_index("ctx")
    h = lax.axis_index("head")
    odd = c % 2 == 1
    even = c % 2 == 0
    partner = (c + 1 - 2 * (c % 2), h)
    per, width, rows = q_hbm.shape
    rank = gf.shape[1]
    flat_rows = rows * per
    keys = WINDOW * rows
    f32, bf16 = jnp.float32, jnp.bfloat16

    def remote(src, dst_ref, ssem, rsem, peer):
        return pltpu.make_async_remote_copy(
            src_ref=src, dst_ref=dst_ref, send_sem=ssem, recv_sem=rsem,
            device_id=peer, device_id_type=pl.DeviceIdType.MESH,
        )

    def arrived(ref, sem):
        remote(ref, ref, sem, sem, partner).wait_recv()

    def sent(ref, sem):
        remote(ref, ref, sem, sem, partner).wait_send()

    load_q = pltpu.make_async_copy(q_hbm, q3, io_sem.at[0])
    load_g = pltpu.make_async_copy(g_hbm, g3, io_sem.at[1])
    load_g.start()
    load_q.start()

    up2, down2 = c + 2 < n, c >= 2
    up3, down3 = odd & (c + 3 < n), even & (c >= 3)
    peers = [(None, (c, (h + k) % heads)) for k in range(1, heads)]
    peers += [(None, partner), (up2, (c + 2, h)), (down2, (c - 2, h)),
              (up3, (c + 3, h)), (down3, (c - 3, h))]
    barrier = pltpu.get_barrier_semaphore()
    for cond, peer in peers:
        @when(cond)
        def _():
            pl.semaphore_signal(
                barrier, inc=1, device_id=peer, device_id_type=pl.DeviceIdType.MESH
            )
    flags = [cond for cond, _ in peers if cond is not None]
    pl.semaphore_wait(barrier, len(peers) - len(flags) + sum(f.astype(jnp.int32) for f in flags))

    def onward(src, s):
        @pl.when(up2)
        def _():
            remote(src, kv.at[BACK2, s], g_send.at[1, s], g_recv.at[BACK2, s], (c + 2, h)).start()

        @pl.when(up3)
        def _():
            remote(src, kv.at[BACK3, s], g_send.at[2, s], g_recv.at[BACK3, s], (c + 3, h)).start()

        @pl.when(even)
        def _():
            remote(src, kv.at[BACK1, s], g_send.at[2, s], g_recv.at[BACK1, s], partner).start()

    def relay(s):
        @pl.when(down2)
        def _():
            arrived(kv.at[BACK2, s], g_recv.at[BACK2, s])

            @pl.when(even)
            def _():
                remote(kv.at[BACK2, s], kv.at[BACK3, s], g_send.at[3, s], g_recv.at[BACK3, s], partner).start()

            @pl.when(odd)
            def _():
                remote(kv.at[BACK2, s], kv.at[BACK1, s], g_send.at[3, s], g_recv.at[BACK1, s], partner).start()

    for k in range(1, heads):
        remote(lat_ref, kv.at[OWN, h], g_send.at[0, k], g_recv.at[OWN, h], (c, (h + k) % heads)).start()
    onward(lat_ref, h)
    kv[OWN, h] = lat_ref[...]

    for place, cond in ((BACK1, c < 1), (BACK2, c < 2), (BACK3, c < 3)):
        @pl.when(cond)
        def _():
            kv[place] = jnp.zeros(kv.shape[1:], kv.dtype)

    load_g.wait()
    lanes = gw.shape[2]
    for i in range(rank // lanes):
        part = pl.ds(i * lanes, lanes)
        gw[i] = g3[:, :, part].astype(f32).reshape(flat_rows, lanes)
        for j in range(per):
            gf[pl.ds(j * rows, rows), part] = gw[i, pl.ds(j, rows, stride=per), :].astype(bf16)

    for k in range(1, heads):
        s = (h + heads - k) % heads
        arrived(kv.at[OWN, s], g_recv.at[OWN, s])
        onward(kv.at[OWN, s], s)
        relay((s + 1) % heads)
    relay((h + 1) % heads)

    load_q.wait()
    for j in range(per):
        qf[:, pl.ds(j * rows, rows)] = q3[j]

    for place, distance in enumerate(DISTANCE):
        row = seg_ref[pl.ds(jnp.maximum(c - distance, 0), 1), :].astype(f32)
        row = jnp.where(c >= distance, row, -1.0)
        kseg[pl.ds(place * rows, rows), :] = jnp.broadcast_to(row, (rows, rows)).T
    qseg = seg_ref[pl.ds(c, 1), :].astype(f32)
    key_at = lax.broadcasted_iota(jnp.int32, (keys, rows), 0) - OWN * rows
    token_at = lax.broadcasted_iota(jnp.int32, (keys, rows), 1)
    allow[...] = ((kseg[...] == qseg) & (key_at <= token_at)).astype(f32)

    for s in range(heads):
        @pl.when(c >= 1)
        def _():
            arrived(kv.at[BACK1, s], g_recv.at[BACK1, s])

        @pl.when(c >= 3)
        def _():
            arrived(kv.at[BACK3, s], g_recv.at[BACK3, s])
    kf[...] = flat(kv[...], keys)

    nt = (((1,), (1,)), ((), ()))
    tn = (((0,), (0,)), ((), ()))
    cols = rows * 2
    for start in range(0, flat_rows, cols):
        part = pl.ds(start, cols)
        st = score_scale * jnp.dot(kf[...], qf[:, part], preferred_element_type=f32)
        gt = lax.dot_general(kf[:, :rank], gf[part, :], nt, preferred_element_type=f32)
        allowed = jnp.concatenate([allow[...]] * (cols // rows), axis=1) > 0.0
        st = jnp.where(allowed, st, -1e30)
        top = jnp.max(st, axis=0, keepdims=True)
        w = jnp.where(allowed, jnp.exp(st - top), 0.0)
        probs = w * (1.0 / jnp.sum(w, axis=0, keepdims=True))
        pt[:, part] = probs.astype(bf16)
        delta = jnp.sum(probs * gt, axis=0, keepdims=True)
        dst[:, part] = (probs * (gt - delta)).astype(bf16)

    def key_grads(first):
        part = pl.ds(first * rows, 2 * rows)
        from_scores = lax.dot_general(dst[part, :], qf[...], nt, preferred_element_type=f32)
        from_values = jnp.dot(pt[part, :], gf[...], preferred_element_type=f32)
        total = jnp.concatenate(
            [score_scale * from_scores[:, :rank] + from_values, score_scale * from_scores[:, rank:]],
            axis=1,
        )
        dk[pl.ds(first, 2)] = total.reshape((2,) + dk.shape[1:])

    order = [(h + k) % heads for k in range(1, heads + 1)]
    key_grads(BACK3)
    sb[pl.ds(BACK3, 2)] = dk[pl.ds(BACK3, 2)].astype(bf16)
    for s in order:
        @pl.when(even & down2)
        def _():
            remote(sb.at[BACK1, s], rp.at[0, s], r_send.at[0, s], r_recv.at[0, s], partner).start()

        @pl.when(odd & (c >= 3))
        def _():
            remote(sb.at[BACK3, s], rp.at[0, s], r_send.at[0, s], r_recv.at[0, s], partner).start()

        @pl.when(odd)
        def _():
            remote(sb.at[BACK1, s], rp.at[1, s], r_send.at[1, s], r_recv.at[1, s], partner).start()

        @pl.when(down3)
        def _():
            remote(sb.at[BACK3, s], r3.at[s], r_send.at[1, s], r_recv.at[3, s], (c - 3, h)).start()
    key_grads(BACK2)
    for s in order:
        @pl.when(down2)
        def _():
            arrived(rp.at[0, s], r_recv.at[0, s])
            sb[BACK2, s] = (dk[BACK2, s] + rp[0, s].astype(f32)).astype(bf16)
            remote(sb.at[BACK2, s], r2.at[s], r_send.at[2, s], r_recv.at[2, s], (c - 2, h)).start()

    for start in range(0, flat_rows, cols):
        dq = score_scale * lax.dot_general(kf[...], dst[:, pl.ds(start, cols)], tn, preferred_element_type=f32)
        for j in range(cols // rows):
            dq3[start // rows + j] = dq[:, j * rows:(j + 1) * rows].astype(bf16)

    for k, s in enumerate(order):
        @pl.when(even)
        def _():
            arrived(rp.at[1, s], r_recv.at[1, s])
            dk[OWN, s] += rp[1, s].astype(f32)

        @pl.when(up2)
        def _():
            arrived(r2.at[s], r_recv.at[2, s])
            dk[OWN, s] += r2[s].astype(f32)

        @pl.when(up3)
        def _():
            arrived(r3.at[s], r_recv.at[3, s])
            dk[OWN, s] += r3[s].astype(f32)

        if k < heads - 1:
            sb[OWN, s] = dk[OWN, s].astype(bf16)
            remote(sb.at[OWN, s], zb.at[h], r_send.at[3, s], r_recv.at[4, h], (c, s)).start()
    total = dk[OWN, h]
    for s in order[-2::-1]:
        arrived(zb.at[s], r_recv.at[4, s])
        total = total + zb[s].astype(f32)
    dlat_ref[...] = total

    shard = zb.at[0]
    for k in range(1, heads):
        sent(lat_ref, g_send.at[0, k])
        sent(shard, r_send.at[3, order[k - 1]])
    for s in range(heads):
        for cond, sem in (
            (up2, g_send.at[1, s]), (up3, g_send.at[2, s]), (even, g_send.at[2, s]),
            (down2, g_send.at[3, s]), (even & down2, r_send.at[0, s]), (odd & (c >= 3), r_send.at[0, s]),
            (odd, r_send.at[1, s]), (down3, r_send.at[1, s]), (down2, r_send.at[2, s]),
        ):
            @pl.when(cond)
            def _():
                sent(shard, sem)


def store_kernel(dq_in, dlat_in, dq_hbm, dlat_hbm, dq_ref, dlat_ref, sems):
    count = dq_ref.shape[0]
    pieces = [(dlat_in, dlat_ref, dlat_hbm)]
    for j in range(count):
        pieces.append((dq_in.at[j], dq_ref.at[j], dq_hbm.at[j]))
    loads = [pltpu.make_async_copy(p[0], p[1], sems.at[0, i]) for i, p in enumerate(pieces)]
    stores = [pltpu.make_async_copy(p[1], p[2], sems.at[1, i]) for i, p in enumerate(pieces)]
    for load in loads:
        load.start()
    for load, store in zip(loads, stores):
        load.wait()
        store.start()
    for store in stores:
        store.wait()


def shards(n, heads, queries, latent, out_grad, segments):
    rows, per, width = queries.shape
    rank = out_grad.shape[2]
    height = latent.shape[0]
    f32, bf16 = jnp.float32, jnp.bfloat16
    flat_rows, keys = rows * per, WINDOW * rows
    vmem = pl.BlockSpec(memory_space=pltpu.VMEM)
    hbm = pl.BlockSpec(memory_space=pltpu.HBM)
    query_grad, latent_grad = pl.pallas_call(
        functools.partial(kernel, n, heads),
        out_shape=(
            jax.ShapeDtypeStruct((per, width, rows), bf16),
            jax.ShapeDtypeStruct(latent.shape, f32),
        ),
        in_specs=[hbm, vmem, hbm, vmem],
        out_specs=(vmem, vmem),
        scratch_shapes=[
            pltpu.VMEM((per, width, rows), bf16),
            pltpu.VMEM((rows, per, rank), bf16),
            pltpu.VMEM((rank // 128, flat_rows, 128), f32),
            pltpu.VMEM((width, flat_rows), bf16),
            pltpu.VMEM((flat_rows, rank), bf16),
            pltpu.VMEM((WINDOW, heads, height, width), bf16),
            pltpu.VMEM((keys, width), bf16),
            pltpu.VMEM((keys, rows), f32),
            pltpu.VMEM((keys, rows), f32),
            pltpu.VMEM((keys, flat_rows), bf16),
            pltpu.VMEM((keys, flat_rows), bf16),
            pltpu.VMEM((WINDOW, heads, height, width), f32),
            pltpu.VMEM((WINDOW, heads, height, width), bf16),
            pltpu.VMEM((2, heads, height, width), bf16),
            pltpu.VMEM((heads, height, width), bf16),
            pltpu.VMEM((heads, height, width), bf16),
            pltpu.VMEM((heads, height, width), bf16),
            pltpu.SemaphoreType.DMA((2,)),
            pltpu.SemaphoreType.DMA((4, heads)),
            pltpu.SemaphoreType.DMA((4, heads)),
            pltpu.SemaphoreType.DMA((4, heads)),
            pltpu.SemaphoreType.DMA((5, heads)),
        ],
        compiler_params=pltpu.CompilerParams(
            collective_id=0, has_side_effects=True, vmem_limit_bytes=67043328
        ),
    )(queries.transpose(1, 2, 0), latent, out_grad, segments.reshape(-1, rows))
    query_grad, latent_grad = pl.pallas_call(
        store_kernel,
        out_shape=(
            jax.ShapeDtypeStruct(query_grad.shape, bf16),
            jax.ShapeDtypeStruct(latent.shape, f32),
        ),
        in_specs=[hbm, hbm],
        out_specs=(hbm, hbm),
        scratch_shapes=[
            pltpu.VMEM((per, width, rows), bf16),
            pltpu.VMEM(latent.shape, f32),
            pltpu.SemaphoreType.DMA((2, per + 1)),
        ],
        compiler_params=pltpu.CompilerParams(vmem_limit_bytes=67043328),
    )(query_grad, latent_grad)
    return query_grad.transpose(2, 0, 1), latent_grad


def solution(mesh):
    n, heads = mesh.shape["ctx"], mesh.shape["head"]
    in_specs = (P("ctx", "head", None), P(("ctx", "head"), None), P("ctx", "head", None), P())
    out_specs = (P("ctx", "head", None), P(("ctx", "head"), None))
    return jax.shard_map(
        functools.partial(shards, n, heads),
        mesh=mesh, in_specs=in_specs, out_specs=out_specs, check_vma=False,
    )
```
